512 devices in a mesh: section: 2 (over y_lo), sample: 16 (over z, core), seq: 16 (over x, y_hi).
Axes of the slice: x: 4, y: 8 (y_hi: 4, y_lo: 2; y = y_hi * 2 + y_lo), z: 8, core: 2. Of those that a mesh axis runs over, the one named last changes fastest.
Arguments:
- first_rows: bfloat16 [2, 16, 2048, 2048], P('section', 'sample', 'seq'), may hold values from -10 to 10
- second_rows: bfloat16 [2, 16, 2048, 2048], P('section', 'sample', 'seq'), may hold values from -6 to 6
- alignment: int32 [16, 16, 2], P('sample', 'seq'), may hold values from 0 to 15, as said below
- diffusion_mask: int32 [16, 2048], P('sample', 'seq'), may hold values 0 or 1
- source_length: int32 [16], P('sample'), may hold values from 1024 to 2048, as said below
- target_length: int32 [16], P('sample'), may hold values from 1024 to 2048
Outputs:
- grad_first: bfloat16 [2, 16, 2048, 2048], P('section', 'sample', 'seq')
- grad_second: bfloat16 [2, 16, 2048, 2048], P('section', 'sample', 'seq')
The draws below stay inside these ranges and needn't reach their ends.
Inputs may be any that keep to these rules, and one draw needn't show every extreme that they name: `alignment`: each list names 2 different blocks from t - 1 to t + 1 for target block t; where block t holds a target position below the target length, every listed block starts below the source length. `source_length`: at least the sample's target length.
All inputs are finite; a program needn't handle non-finite values. No bound on the sum of `diffusion_mask` on one device may be relied on, other than what follows from the above.
Results may differ from the reference program's by a relative error of at most 0.013.
Values may be sent and summed in bfloat16 or wider, within the bound.
A program may use at most 64 MiB of HBM per device.

```python
import jax
import jax.numpy as jnp
from jax import lax

HEADS = 32
HDIM = 64
INNER = 2048
BLK = 128
NLIST = 2
WIN = 1
SAMPLES = 16
SEQLEN = 2048
NBLK = 16


def plan_integers(key):
    base = jax.random.fold_in(key, 4099)
    key_target, key_order, key_spread, key_lists = jax.random.split(base, 4)
    sample_ids = jnp.arange(SAMPLES, dtype=jnp.int32)
    target_len = jax.random.randint(key_target, (SAMPLES,), SEQLEN // 2, SEQLEN + 1)
    order = jax.random.permutation(key_order, SAMPLES)
    longest = order[0]
    shortest = order[1]
    target_len = jnp.where(sample_ids == longest, SEQLEN, target_len)
    target_len = jnp.where(sample_ids == shortest, SEQLEN // 2, target_len)
    spread = jax.random.randint(key_spread, (SAMPLES,), 0, 1 << 20)
    source_len = target_len + spread % (SEQLEN - target_len + 1)
    source_len = jnp.where(sample_ids == shortest, target_len, source_len)
    valid_blocks = (source_len + BLK - 1) // BLK
    blocks = jnp.arange(NBLK, dtype=jnp.int32)
    width = 2 * WIN + 1
    offsets = jnp.arange(width, dtype=jnp.int32) - WIN
    candidate = blocks[:, None] + offsets[None, :]
    in_range = (candidate >= 0) & (candidate < NBLK)
    holds_rows = blocks[None, :] * BLK < target_len[:, None]
    allowed = in_range[None, :, :] & (~holds_rows[:, :, None] | (candidate[None, :, :] < valid_blocks[:, None, None]))
    noise = jax.random.randint(key_lists, (SAMPLES, NBLK, width), 0, 1 << 20) * width + offsets[None, None, :] + WIN
    ranking = jnp.where(allowed, noise, -1)
    unused, picks = lax.top_k(ranking, NLIST)
    lists = blocks[None, :, None] + picks.astype(jnp.int32) - WIN
    return (lists.astype(jnp.int32), source_len.astype(jnp.int32), target_len.astype(jnp.int32))


def draw_alignment(key, part):
    return plan_integers(key)[0]


def draw_source_length(key, part):
    return plan_integers(key)[1]


def draw_target_length(key, part):
    return plan_integers(key)[2]


def draw_first_rows(key, part):
    key_base = jax.random.fold_in(jax.random.fold_in(key, 17), 0)
    shape = (2, SAMPLES, SEQLEN, INNER)
    base = jnp.clip(jax.random.normal(key_base, shape, jnp.float32), -4.0, 4.0)
    return base.astype(jnp.bfloat16)


def with_ends(values, stream_key, least, high):
    place = [jax.random.randint(jax.random.fold_in(stream_key, axis), (), 0, length) for axis, length in enumerate(values.shape)]
    main_axis = values.shape.index(max(values.shape))
    next_to = place[:main_axis] + [(place[main_axis] + 1) % values.shape[main_axis]] + place[main_axis + 1:]
    return values.at[tuple(place)].set(least).at[tuple(next_to)].set(high)


def steps_of(own_key, shape, cuts, smallest, high):
    def one(position, blocks):
        draws = jax.random.uniform(jax.random.fold_in(jax.random.fold_in(own_key, 6), position), (blocks,), jnp.float32, smallest / len(cuts), high / len(cuts))
        return jnp.repeat(jnp.exp(draws), shape[position] // blocks).reshape((-1,) + (1,) * (len(shape) - position - 1))

    gain = one(*cuts[0])
    for cut in cuts[1:]:
        gain = gain * one(*cut)
    return gain


def gaussian(own_key, extent, scale, bound, pieces=(), kind=jnp.bfloat16):
    values = jax.random.normal(own_key, extent, jnp.float32) * scale
    if len(pieces) > 0:
        values = steps_of(own_key, extent, pieces, -0.22, 0.18) * values
    return jnp.clip(values, min=-bound, max=bound).astype(kind)


def setup_inputs(seed: int = 0) -> dict:
    key_list = jax.random.split(jax.random.key(seed), 7)
    first_rows = draw_first_rows(jax.random.fold_in(key_list[6], 71), 0)
    second_rows = gaussian(key_list[1], (2, SAMPLES, SEQLEN, INNER), 1.0, 6.0, ((0, 2), (1, 16), (2, 16)))
    alignment = draw_alignment(jax.random.fold_in(key_list[6], 71), 0)
    diffusion_mask = with_ends((jax.random.randint(key_list[3], (SAMPLES, SEQLEN), 0, 2) < 1).astype(jnp.int32), jax.random.fold_in(key_list[3], 1), 0, 1)
    source_length = draw_source_length(jax.random.fold_in(key_list[6], 71), 0)
    target_length = draw_target_length(jax.random.fold_in(key_list[6], 71), 0)
    return dict(first_rows=first_rows, second_rows=second_rows, alignment=alignment, diffusion_mask=diffusion_mask, source_length=source_length, target_length=target_length)


NEG_FILL = -1e30


def attend_block(query_blk, cot_blk, key_rows, value_rows, key_valid, query_valid, cot_keep):
    scale = HDIM ** -0.5
    queries = query_blk.reshape(BLK, HEADS, HDIM).astype(jnp.float32)
    keys = key_rows.reshape(NLIST * BLK, HEADS, HDIM).astype(jnp.float32)
    values = value_rows.reshape(NLIST * BLK, HEADS, HDIM).astype(jnp.float32)
    scores = jnp.einsum("qhd,khd->hqk", queries, keys) * scale
    scores = jnp.where(key_valid[None, None, :], scores, NEG_FILL)
    peak = jnp.max(scores, axis=-1, keepdims=True)
    expo = jnp.exp(scores - peak)
    probs = expo / jnp.sum(expo, axis=-1, keepdims=True)
    probs_low = lax.optimization_barrier(probs.astype(jnp.bfloat16)).astype(jnp.float32)
    attended = jnp.einsum("hqk,khd->qhd", probs_low, values)
    attended = jnp.where(query_valid[:, None, None], attended, jnp.float32(0.0))
    out_low = attended.astype(jnp.bfloat16)
    out_wide = lax.optimization_barrier(out_low).astype(jnp.float32)
    cot = jnp.where(cot_keep[:, None], cot_blk, jnp.zeros_like(cot_blk))
    cot_wide = cot.reshape(BLK, HEADS, HDIM).astype(jnp.float32)
    delta = jnp.sum(cot_wide * out_wide, axis=-1).T[:, :, None]
    dprob = jnp.einsum("qhd,khd->hqk", cot_wide, values)
    dscore = probs * (dprob - delta)
    dscore_low = lax.optimization_barrier(dscore.astype(jnp.bfloat16)).astype(jnp.float32)
    dvalue = jnp.einsum("hqk,qhd->khd", probs_low, cot_wide)
    dquery = scale * jnp.einsum("hqk,khd->qhd", dscore_low, keys)
    dkey = scale * jnp.einsum("hqk,qhd->khd", dscore_low, queries)
    return (out_low.reshape(BLK, INNER), dquery.astype(jnp.bfloat16).reshape(BLK, INNER),
            dkey.reshape(NLIST, BLK, INNER), dvalue.reshape(NLIST, BLK, INNER))


def one_sample(first_pair, second_pair, lists, mask_row, source_len, target_len):
    key_blocks = first_pair[0].reshape(NBLK, BLK, INNER)
    query_blocks = first_pair[1].reshape(NBLK, BLK, INNER)
    value_blocks = second_pair[0].reshape(NBLK, BLK, INNER)
    cot_blocks = second_pair[1].reshape(NBLK, BLK, INNER)
    mask_blocks = mask_row.reshape(NBLK, BLK)
    inside = jnp.arange(BLK, dtype=jnp.int32)

    def step(carry, index):
        key_acc, value_acc = carry
        chosen = lists[index]
        key_rows = key_blocks[chosen].reshape(NLIST * BLK, INNER)
        value_rows = value_blocks[chosen].reshape(NLIST * BLK, INNER)
        key_pos = (chosen[:, None] * BLK + inside[None, :]).reshape(NLIST * BLK)
        key_valid = key_pos < source_len
        row_pos = index * BLK + inside
        query_valid = row_pos < target_len
        cot_keep = query_valid & (mask_blocks[index] == 1)
        out_low, dquery, dkey, dvalue = attend_block(query_blocks[index], cot_blocks[index], key_rows,
                                                     value_rows, key_valid, query_valid, cot_keep)
        key_acc = key_acc.at[chosen].add(dkey)
        value_acc = value_acc.at[chosen].add(dvalue)
        return (key_acc, value_acc), (out_low, dquery)

    start = (jnp.zeros((NBLK, BLK, INNER), jnp.float32), jnp.zeros((NBLK, BLK, INNER), jnp.float32))
    (key_acc, value_acc), (outs, dqueries) = lax.scan(step, start, jnp.arange(NBLK, dtype=jnp.int32))
    return (key_acc.reshape(SEQLEN, INNER).astype(jnp.bfloat16), dqueries.reshape(SEQLEN, INNER),
            value_acc.reshape(SEQLEN, INNER).astype(jnp.bfloat16), outs.reshape(SEQLEN, INNER))


def reference(first_rows, second_rows, alignment, diffusion_mask, source_length, target_length):
    firsts = jnp.moveaxis(first_rows, 1, 0)
    seconds = jnp.moveaxis(second_rows, 1, 0)

    def per_sample(packed):
        return one_sample(packed[0], packed[1], packed[2], packed[3], packed[4], packed[5])

    key_grad, query_grad, value_grad, outs = lax.map(
        per_sample, (firsts, seconds, alignment, diffusion_mask, source_length, target_length))
    return jnp.stack([key_grad, query_grad], 0), jnp.stack([value_grad, outs], 0)
```

```python
import functools

import jax
import jax.numpy as jnp
from jax import lax
from jax.experimental import pallas as pl
from jax.experimental.pallas import tpu as pltpu
from jax.sharding import PartitionSpec as P

HDIM = 64
BLK = 128
CW = 256
LANES = 128
SCALE = HDIM**-0.5
LOG2E = 1.4426950408889634
BIG = 1e30
MESH = pl.DeviceIdType.MESH
NT = (((1,), (1,)), ((), ()))
NN = (((1,), (0,)), ((), ()))


def dot(a, b, dims):
    return lax.dot_general(a, b, dims, preferred_element_type=jnp.float32)


def kernel(
    count,
    align,
    source_len,
    target_len,
    mask,
    first,
    second,
    grad_first,
    grad_second,
    own,
    recv,
    outs,
    keep_rows,
    stat_out,
    stat_in,
    own_sem,
    send_sem,
    recv_sem,
    relay_send,
    relay_recv,
    stat_send,
    stat_recv,
    out_sem,
):
    width = first.shape[-1]
    chunks = width // CW
    heads = CW // HDIM
    section = lax.axis_index("section")
    seq = lax.axis_index("seq")
    step = 2 * section - 1
    ahead = lax.rem(seq + step + count, count)
    behind = lax.rem(seq - step + count, count)
    partner = {"section": 1 - section, "seq": seq}
    side = {"section": 1 - section, "seq": ahead}
    far = {"section": 1 - section, "seq": behind}
    relay_to = {"section": section, "seq": ahead}
    relay_from = {"section": section, "seq": behind}

    inputs = (first, second)
    results = (grad_first, grad_second)

    def columns(c):
        return pl.ds(pl.multiple_of(c * CW, CW), CW)

    def own_copy(arr):
        return pltpu.make_async_copy(inputs[arr].at[0, 0], own.at[arr], own_sem.at[arr])

    def block_copy(slot, arr, c):
        return pltpu.make_async_remote_copy(
            src_ref=inputs[arr].at[0, 0, :, columns(c)],
            dst_ref=recv.at[slot, arr, :, columns(c)],
            send_sem=send_sem.at[slot, arr, c],
            recv_sem=recv_sem.at[slot, arr, c],
            device_id=(partner, side)[slot],
            device_id_type=MESH,
        )

    def relay_copy(c):
        return pltpu.make_async_remote_copy(
            src_ref=recv.at[0, :, :, columns(c)],
            dst_ref=recv.at[2, :, :, columns(c)],
            send_sem=relay_send.at[c],
            recv_sem=relay_recv.at[c],
            device_id=relay_to,
            device_id_type=MESH,
        )

    def stat_copy(slot, c):
        return pltpu.make_async_remote_copy(
            src_ref=stat_out.at[slot, c],
            dst_ref=stat_in.at[slot, c],
            send_sem=stat_send.at[slot, c],
            recv_sem=stat_recv.at[slot, c],
            device_id=(partner, side, far)[slot],
            device_id_type=MESH,
        )

    def out_copy(arr, c):
        return pltpu.make_async_copy(
            outs.at[arr, :, columns(c)],
            results[arr].at[0, 0, :, columns(c)],
            out_sem.at[arr, c],
        )

    for arr in range(2):
        own_copy(arr).start()

    barrier = pltpu.get_barrier_semaphore()
    for peer in (partner, side, far, relay_to, relay_from):
        pl.semaphore_signal(barrier, inc=1, device_id=peer, device_id_type=MESH)
    pl.semaphore_wait(barrier, 5)

    def send_own(c, carry):
        for slot in range(2):
            for arr in range(2):
                block_copy(slot, arr, c).start()
        return carry

    lax.fori_loop(0, chunks, send_own, 0)

    def relay(c):
        for arr in range(2):
            block_copy(0, arr, c).wait_recv()
        relay_copy(c).start()

    for arr in range(2):
        own_copy(arr).wait()

    lane = lax.broadcasted_iota(jnp.int32, (1, LANES), 1)
    row = lax.broadcasted_iota(jnp.int32, (BLK, LANES), 0)
    low_half = lane < HDIM
    half_mask = (
        low_half.astype(jnp.float32).astype(jnp.bfloat16),
        (1.0 - low_half.astype(jnp.float32)).astype(jnp.bfloat16),
    )
    limit = target_len[0]
    source_end = source_len[0]

    @pl.when(section == 1)
    def _():
        missing = 2 * seq - align[0, 0, 0] - align[0, 0, 1]
        lower_missing = missing == -1
        upper_missing = missing == 1
        first_block = jnp.where(lower_missing, seq, seq - 1)
        second_block = jnp.where(upper_missing, seq, seq + 1)
        key_pos = jnp.concatenate([first_block * BLK + lane, second_block * BLK + lane], axis=1)
        key_valid = key_pos < source_end
        live_lane = (seq * BLK + lane < limit).astype(jnp.float32)
        keep_lane = live_lane * (mask[...] == 1).astype(jnp.float32)
        keep_rows[...] = jnp.broadcast_to(keep_lane, (BLK, LANES)).T
        listed = tuple(
            jnp.where(missing == offset, jnp.float32(0.0), jnp.float32(1.0)) for offset in (0, 1, -1)
        )
        stat_lane = lax.broadcasted_iota(jnp.int32, (BLK, LANES), 1)
        stat_row = lax.broadcasted_iota(jnp.int32, (2 * heads, LANES), 0)

        relay(0)
        relay(1)

        def body(c, carry):
            for arr in range(2):
                block_copy(1, arr, c).wait_recv()
            relay_copy(c).wait_recv()
            live = seq * BLK + row < limit
            stats = jnp.zeros((BLK, LANES), jnp.float32)
            saved = []
            for pair in range(CW // LANES):
                cols = pl.ds(pl.multiple_of(c * CW + pair * LANES, LANES), LANES)
                query = own[0, :, cols]
                cot = own[1, :, cols]
                kv = []
                for arr in range(2):
                    middle = recv[0, arr, :, cols]
                    lower = lax.select(lower_missing, middle, recv[2, arr, :, cols])
                    upper = lax.select(upper_missing, middle, recv[1, arr, :, cols])
                    kv.append(jnp.concatenate([lower, upper], axis=0))
                keys, values = kv
                halves = []
                for half in range(2):
                    head = 2 * pair + half
                    cot_half = cot * half_mask[half]
                    scores = dot(query * half_mask[half], keys, NT) * (SCALE * LOG2E)
                    scores = jnp.where(key_valid, scores, -BIG)
                    peak = jnp.max(scores, axis=-1, keepdims=True)
                    expo = jnp.exp2(scores - peak)
                    total = jnp.sum(expo, axis=-1, keepdims=True)
                    probs = expo * (1.0 / total)
                    attended = dot(probs.astype(jnp.bfloat16), values, NN)
                    out_low = jnp.where(live, attended, 0.0).astype(jnp.bfloat16).astype(jnp.float32)
                    delta = jnp.sum(cot_half.astype(jnp.float32) * out_low, axis=-1, keepdims=True)
                    lse = peak + jnp.log(total) * LOG2E
                    stats = jnp.where(stat_lane == head, lse, stats)
                    stats = jnp.where(stat_lane == heads + head, delta, stats)
                    halves.append(out_low)
                    saved.append((cot_half, keys, values, probs, delta))
                outs[1, :, cols] = jnp.where(low_half, halves[0], halves[1]).astype(jnp.bfloat16)
            stats = stats.T[: 2 * heads]
            for slot in range(3):
                kept = keep_lane * listed[slot]
                stat_out[slot, c] = jnp.where((stat_row >= heads) | (kept == 1.0), stats, BIG)
            for slot in range(3):
                stat_copy(slot, c).start()

            @pl.when(c + 2 < chunks)
            def _():
                relay(c + 2)

            out_copy(1, c).start()
            for pair in range(CW // LANES):
                cols = pl.ds(pl.multiple_of(c * CW + pair * LANES, LANES), LANES)
                halves = []
                for half in range(2):
                    cot_half, keys, values, probs, delta = saved[2 * pair + half]
                    dprob = dot(cot_half, values, NT)
                    dscore = (probs * (dprob - delta)).astype(jnp.bfloat16)
                    halves.append(dot(dscore, keys, NN))
                dquery = jnp.where(low_half, halves[0], halves[1]) * SCALE
                dquery = jnp.where(keep_rows[...] == 1.0, dquery, 0.0)
                outs[0, :, cols] = dquery.astype(jnp.bfloat16)
            out_copy(0, c).start()
            return carry

        lax.fori_loop(0, chunks, body, 0)

        def drain(c, carry):
            for slot in range(3):
                stat_copy(slot, c).wait_send()
            return carry

        lax.fori_loop(0, chunks, drain, 0)

    @pl.when(section == 0)
    def _():
        def relay_all(c, carry):
            relay(c)
            return carry

        lax.fori_loop(0, chunks, relay_all, 0)

        def body(c, carry):
            for arr in range(2):
                block_copy(1, arr, c).wait_recv()
            relay_copy(c).wait_recv()
            for slot in range(3):
                stat_copy(slot, c).wait_recv()
            valid = seq * BLK + row < source_end
            stats = jnp.concatenate([stat_in[slot, c] for slot in range(3)], axis=1)
            for pair in range(CW // LANES):
                cols = pl.ds(pl.multiple_of(c * CW + pair * LANES, LANES), LANES)
                keys = own[0, :, cols]
                values = own[1, :, cols]
                queries = recv[:, 0, :, cols].reshape(3 * BLK, LANES)
                cots = recv[:, 1, :, cols].reshape(3 * BLK, LANES)
                key_halves = []
                value_halves = []
                for half in range(2):
                    head = 2 * pair + half
                    scores = dot(keys * half_mask[half], queries, NT) * (SCALE * LOG2E)
                    probs = jnp.exp2(scores - stats[head : head + 1])
                    dprob = dot(values * half_mask[half], cots, NT)
                    dscore = probs * (dprob - stats[heads + head : heads + head + 1])
                    value_halves.append(dot(probs.astype(jnp.bfloat16), cots, NN))
                    key_halves.append(dot(dscore.astype(jnp.bfloat16), queries, NN))
                dkey = jnp.where(low_half, key_halves[0], key_halves[1]) * SCALE
                dvalue = jnp.where(low_half, value_halves[0], value_halves[1])
                outs[0, :, cols] = jnp.where(valid, dkey, 0.0).astype(jnp.bfloat16)
                outs[1, :, cols] = jnp.where(valid, dvalue, 0.0).astype(jnp.bfloat16)
            for arr in range(2):
                out_copy(arr, c).start()
            return carry

        lax.fori_loop(0, chunks, body, 0)

    def drain(c, carry):
        for slot in range(2):
            for arr in range(2):
                block_copy(slot, arr, c).wait_send()
        relay_copy(c).wait_send()
        for arr in range(2):
            out_copy(arr, c).wait()
        return carry

    lax.fori_loop(0, chunks, drain, 0)


def on_device(first_rows, second_rows, alignment, diffusion_mask, source_length, target_length):
    count = lax.axis_size("seq")
    width = first_rows.shape[3]
    chunks = width // CW
    heads = CW // HDIM
    shape = jax.ShapeDtypeStruct(first_rows.shape, jnp.bfloat16)
    anywhere = pl.BlockSpec(memory_space=pl.ANY)
    scalars = pl.BlockSpec(memory_space=pltpu.SMEM)
    return pl.pallas_call(
        functools.partial(kernel, count),
        out_shape=(shape, shape),
        in_specs=[
            scalars,
            scalars,
            scalars,
            pl.BlockSpec(memory_space=pltpu.VMEM),
            anywhere,
            anywhere,
        ],
        out_specs=(anywhere, anywhere),
        scratch_shapes=[
            pltpu.VMEM((2, BLK, width), jnp.bfloat16),
            pltpu.VMEM((3, 2, BLK, width), jnp.bfloat16),
            pltpu.VMEM((2, BLK, width), jnp.bfloat16),
            pltpu.VMEM((BLK, LANES), jnp.float32),
            pltpu.VMEM((3, chunks, 2 * heads, BLK), jnp.float32),
            pltpu.VMEM((3, chunks, 2 * heads, BLK), jnp.float32),
            pltpu.SemaphoreType.DMA((2,)),
            pltpu.SemaphoreType.DMA((2, 2, chunks)),
            pltpu.SemaphoreType.DMA((2, 2, chunks)),
            pltpu.SemaphoreType.DMA((chunks,)),
            pltpu.SemaphoreType.DMA((chunks,)),
            pltpu.SemaphoreType.DMA((3, chunks)),
            pltpu.SemaphoreType.DMA((3, chunks)),
            pltpu.SemaphoreType.DMA((2, chunks)),
        ],
        compiler_params=pltpu.CompilerParams(collective_id=0, has_side_effects=True),
    )(alignment, source_length, target_length, diffusion_mask, first_rows, second_rows)


def solution(mesh):
    placed = (
        P("section", "sample", "seq", None),
        P("section", "sample", "seq", None),
        P("sample", "seq", None),
        P("sample", "seq"),
        P("sample"),
        P("sample"),
    )
    return jax.shard_map(
        on_device,
        mesh=mesh,
        in_specs=placed,
        out_specs=(P("section", "sample", "seq", None), P("section", "sample", "seq", None)),
        check_vma=False,
    )
```

```python
import functools

import jax
import jax.numpy as jnp
from jax import lax
from jax.experimental import pallas as pl
from jax.experimental.pallas import tpu as pltpu
from jax.sharding import PartitionSpec as P

HDIM = 64
BLK = 128
CW = 256
OWN = 128
AHEAD = 3
LANES = 128
SCALE = HDIM**-0.5
LOG2E = 1.4426950408889634
BIG = 1e30
MESH = pl.DeviceIdType.MESH
NT = (((1,), (1,)), ((), ()))
NN = (((1,), (0,)), ((), ()))


def dot(a, b, dims):
    return lax.dot_general(a, b, dims, preferred_element_type=jnp.float32)


def kernel(
    count,
    align_in,
    source_len,
    target_len,
    mask_in,
    first,
    second,
    grad_first,
    grad_second,
    align,
    mask,
    own,
    recv,
    keep_rows,
    stat_out,
    stat_in,
    own_sem,
    send_sem,
    recv_sem,
    relay_send,
    relay_recv,
    stat_send,
    stat_recv,
    small_sem,
):
    width = first.shape[-1]
    chunks = width // CW
    heads = CW // HDIM
    section = lax.axis_index("section")
    seq = lax.axis_index("seq")
    step = 2 * section - 1
    ahead = lax.rem(seq + step + count, count)
    behind = lax.rem(seq - step + count, count)
    partner = {"section": 1 - section, "seq": seq}
    side = {"section": 1 - section, "seq": ahead}
    far = {"section": 1 - section, "seq": behind}
    relay_to = {"section": section, "seq": ahead}
    relay_from = {"section": section, "seq": behind}

    inputs = (first, second)

    def columns(c):
        return pl.ds(pl.multiple_of(c * CW, CW), CW)

    def own_copy(arr):
        return pltpu.make_async_copy(inputs[arr].at[0, 0], own.at[arr], own_sem.at[arr])

    def block_copy(slot, arr, g):
        part = pl.ds(pl.multiple_of(g * OWN, OWN), OWN)
        return pltpu.make_async_remote_copy(
            src_ref=inputs[arr].at[0, 0, :, part],
            dst_ref=recv.at[slot, arr, :, part],
            send_sem=send_sem.at[slot, arr, g],
            recv_sem=recv_sem.at[slot, arr, g],
            device_id=(partner, side)[slot],
            device_id_type=MESH,
        )

    def relay_copy(c):
        return pltpu.make_async_remote_copy(
            src_ref=recv.at[0, :, :, columns(c)],
            dst_ref=recv.at[2, :, :, columns(c)],
            send_sem=relay_send.at[c],
            recv_sem=relay_recv.at[c],
            device_id=relay_to,
            device_id_type=MESH,
        )

    def stat_copy(slot, c):
        return pltpu.make_async_remote_copy(
            src_ref=stat_out.at[slot, c],
            dst_ref=stat_in.at[slot, c],
            send_sem=stat_send.at[slot, c],
            recv_sem=stat_recv.at[slot, c],
            device_id=(partner, side, far)[slot],
            device_id_type=MESH,
        )

    has_ahead = (seq + step >= 0) & (seq + step < count)
    has_behind = (seq - step >= 0) & (seq - step < count)

    barrier = pltpu.get_barrier_semaphore()

    def greet(*peers):
        for peer in peers:
            pl.semaphore_signal(barrier, inc=1, device_id=peer, device_id_type=MESH)

    greet(partner)
    pl.when(has_ahead)(lambda: greet(side, relay_to))
    pl.when(has_behind)(lambda: greet(far, relay_from))

    small = [
        pltpu.make_async_copy(src, dst, small_sem.at[i])
        for i, (src, dst) in enumerate(
            ((align_in, align), (mask_in, mask))
        )
    ]
    for copy in small:
        copy.start()
    for arr in range(2):
        own_copy(arr).start()
    pl.semaphore_wait(barrier, 1 + 2 * has_ahead.astype(jnp.int32) + 2 * has_behind.astype(jnp.int32))

    def for_slots(slots, act):
        conditions = (None, has_ahead, has_behind)
        for slot in slots:
            if slot == 0:
                act(slot)
            else:
                pl.when(conditions[slot])(functools.partial(act, slot))

    def send_own(g, carry):
        def act(slot):
            for arr in range(2):
                block_copy(slot, arr, g).start()

        for_slots((0, 1), act)
        return carry

    lax.fori_loop(0, width // OWN, send_own, 0)

    def relay(c):
        for part in range(CW // OWN):
            for arr in range(2):
                block_copy(0, arr, c * (CW // OWN) + part).wait_recv()
        pl.when(has_ahead)(lambda: relay_copy(c).start())

    groups = width // OWN
    waited = jnp.where(has_behind, groups - 1, groups)

    def wait_ahead(g, carry):
        for arr in range(2):
            block_copy(1, arr, g).wait_recv()
        return carry

    pl.when(has_ahead)(lambda: lax.fori_loop(0, waited, wait_ahead, None))

    def relay_some(c, carry):
        relay(c)
        return carry

    lax.fori_loop(0, jnp.where(section == 1, min(AHEAD, chunks), chunks), relay_some, 0)

    for copy in small:
        copy.wait()
    for arr in range(2):
        own_copy(arr).wait()

    lane = lax.broadcasted_iota(jnp.int32, (1, LANES), 1)
    row = lax.broadcasted_iota(jnp.int32, (BLK, LANES), 0)
    low_half = lane < HDIM
    half_mask = (
        low_half.astype(jnp.float32).astype(jnp.bfloat16),
        (1.0 - low_half.astype(jnp.float32)).astype(jnp.bfloat16),
    )

    def stacked(block):
        return jnp.concatenate([block * half_mask[0], block * half_mask[1]], axis=0)

    limit = target_len[0]
    source_end = source_len[0]

    @pl.when(section == 1)
    def _():
        missing = 2 * seq - align[0, 0, 0] - align[0, 0, 1]
        lower_missing = missing == -1
        upper_missing = missing == 1
        first_block = jnp.where(lower_missing, seq, seq - 1)
        second_block = jnp.where(upper_missing, seq, seq + 1)
        key_pos = lane - source_end
        key_pos = jnp.concatenate([first_block * BLK + key_pos, second_block * BLK + key_pos], axis=1)
        key_valid = key_pos < 0
        live_lane = (seq * BLK + lane < limit).astype(jnp.float32)
        keep_lane = live_lane * (mask[...] == 1).astype(jnp.float32)
        keep_rows[...] = jnp.broadcast_to(keep_lane, (BLK, LANES)).T
        listed = tuple(
            jnp.where(missing == offset, jnp.float32(0.0), jnp.float32(1.0)) for offset in (0, 1, -1)
        )
        stat_lane = lax.broadcasted_iota(jnp.int32, (BLK, LANES), 1)
        stat_row = lax.broadcasted_iota(jnp.int32, (2 * heads, LANES), 0)

        def body(c, carry):
            pl.when((c == chunks - 1) & has_ahead)(lambda: lax.fori_loop(waited, groups, wait_ahead, None))
            pl.when(has_behind)(lambda: relay_copy(c).wait_recv())
            live = seq * BLK + jnp.concatenate([row, row], axis=0) < limit
            stats = jnp.zeros((BLK, LANES), jnp.float32)
            saved = []
            for pair in range(CW // LANES):
                cols = pl.ds(pl.multiple_of(c * CW + pair * LANES, LANES), LANES)
                query = own[0, :, cols]
                cot = own[1, :, cols]
                kv = []
                for arr in range(2):
                    middle = recv[0, arr, :, cols]
                    lower = lax.select(lower_missing, middle, recv[2, arr, :, cols])
                    upper = lax.select(upper_missing, middle, recv[1, arr, :, cols])
                    kv.append(jnp.concatenate([lower, upper], axis=0))
                keys, values = kv
                cots = stacked(cot)
                scores = dot(stacked(query), keys, NT) * (SCALE * LOG2E)
                scores = jnp.where(key_valid, scores, -BIG)
                peak = jnp.max(scores, axis=-1, keepdims=True)
                expo = jnp.exp2(scores - peak)
                total = jnp.sum(expo, axis=-1, keepdims=True)
                probs = expo * (1.0 / total)
                attended = dot(probs.astype(jnp.bfloat16), values, NN)
                out_low = jnp.where(live, attended, 0.0).astype(jnp.bfloat16).astype(jnp.float32)
                delta = jnp.sum(cots.astype(jnp.float32) * out_low, axis=-1, keepdims=True)
                lse = peak + jnp.log(total) * LOG2E
                for half in range(2):
                    head = 2 * pair + half
                    rows = slice(half * BLK, (half + 1) * BLK)
                    stats = jnp.where(stat_lane == head, lse[rows], stats)
                    stats = jnp.where(stat_lane == heads + head, delta[rows], stats)
                saved.append((cots, keys, values, probs, delta))
                halves = out_low[:BLK], out_low[BLK:]
                grad_second[0, 0, :, cols] = jnp.where(low_half, halves[0], halves[1]).astype(jnp.bfloat16)
            stats = stats.T[: 2 * heads]
            for slot in range(3):
                kept = keep_lane * listed[slot]
                stat_out[slot, c] = jnp.where((stat_row >= heads) | (kept == 1.0), stats, BIG)
            for_slots((2, 1, 0), lambda slot: stat_copy(slot, c).start())
            pl.when(c + AHEAD < chunks)(lambda: relay(c + AHEAD))

            for pair in range(CW // LANES):
                cols = pl.ds(pl.multiple_of(c * CW + pair * LANES, LANES), LANES)
                cots, keys, values, probs, delta = saved[pair]
                dprob = dot(cots, values, NT)
                dscore = (probs * (dprob - delta)).astype(jnp.bfloat16)
                queries_grad = dot(dscore, keys, NN)
                halves = queries_grad[:BLK], queries_grad[BLK:]
                dquery = jnp.where(low_half, halves[0], halves[1]) * SCALE
                dquery = jnp.where(keep_rows[...] == 1.0, dquery, 0.0)
                grad_first[0, 0, :, cols] = dquery.astype(jnp.bfloat16)
            return carry

        lax.fori_loop(0, chunks, body, 0)

        def drain(c, carry):
            for_slots(range(3), lambda slot: stat_copy(slot, c).wait_send())
            return carry

        lax.fori_loop(0, chunks, drain, 0)

    @pl.when(section == 0)
    def _():
        def absent(slot):
            recv[slot] = jnp.zeros_like(recv[slot])
            stat_in[slot] = jnp.full_like(stat_in[slot], BIG)

        pl.when(jnp.logical_not(has_ahead))(lambda: absent(1))
        pl.when(jnp.logical_not(has_behind))(lambda: absent(2))

        def body(c, carry):
            pl.when((c == chunks - 1) & has_ahead)(lambda: lax.fori_loop(waited, groups, wait_ahead, None))
            pl.when(has_behind)(lambda: relay_copy(c).wait_recv())
            for_slots(range(3), lambda slot: stat_copy(slot, c).wait_recv())
            valid = seq * BLK + row < source_end
            stats = jnp.concatenate([stat_in[slot, c] for slot in range(3)], axis=1)
            for pair in range(CW // LANES):
                cols = pl.ds(pl.multiple_of(c * CW + pair * LANES, LANES), LANES)
                queries = recv[:, 0, :, cols].reshape(3 * BLK, LANES)
                cots = recv[:, 1, :, cols].reshape(3 * BLK, LANES)

                def per_key(base):
                    rows = [stats[base + 2 * pair + half : base + 2 * pair + half + 1] for half in range(2)]
                    return jnp.concatenate([jnp.broadcast_to(line, (BLK, 3 * BLK)) for line in rows], axis=0)

                scores = dot(stacked(own[0, :, cols]), queries, NT) * (SCALE * LOG2E)
                probs = jnp.exp2(scores - per_key(0))
                dprob = dot(stacked(own[1, :, cols]), cots, NT)
                dscore = probs * (dprob - per_key(heads))
                dvalue = dot(probs.astype(jnp.bfloat16), cots, NN)
                dkey = dot(dscore.astype(jnp.bfloat16), queries, NN)
                dkey = jnp.where(low_half, dkey[:BLK], dkey[BLK:]) * SCALE
                dvalue = jnp.where(low_half, dvalue[:BLK], dvalue[BLK:])
                grad_first[0, 0, :, cols] = jnp.where(valid, dkey, 0.0).astype(jnp.bfloat16)
                grad_second[0, 0, :, cols] = jnp.where(valid, dvalue, 0.0).astype(jnp.bfloat16)
            return carry

        lax.fori_loop(0, chunks, body, 0)

    def drain_own(g, carry):
        def act(slot):
            for arr in range(2):
                block_copy(slot, arr, g).wait_send()

        for_slots((0, 1), act)
        return carry

    def drain_relay(c, carry):
        relay_copy(c).wait_send()
        return carry

    lax.fori_loop(0, groups, drain_own, 0)
    pl.when(has_ahead)(lambda: lax.fori_loop(0, chunks, drain_relay, None))


def store(first, second, grad_first, grad_second, sems):
    copies = (
        pltpu.make_async_copy(first, grad_first, sems.at[0]),
        pltpu.make_async_copy(second, grad_second, sems.at[1]),
    )
    for copy in copies:
        copy.start()
    for copy in copies:
        copy.wait()


def on_device(first_rows, second_rows, alignment, diffusion_mask, source_length, target_length):
    count = lax.axis_size("seq")
    width = first_rows.shape[3]
    chunks = width // CW
    heads = CW // HDIM
    shape = jax.ShapeDtypeStruct(first_rows.shape, jnp.bfloat16)
    anywhere = pl.BlockSpec(memory_space=pl.ANY)
    on_chip = pl.BlockSpec(memory_space=pltpu.VMEM)
    in_hbm = pl.BlockSpec(memory_space=pltpu.HBM)
    scalars = pl.BlockSpec(memory_space=pltpu.SMEM)

    def kept(array):
        return pltpu.with_memory_space_constraint(array, pltpu.HBM)

    made = pl.pallas_call(
        functools.partial(kernel, count),
        out_shape=(shape, shape),
        in_specs=[in_hbm, scalars, scalars, in_hbm, in_hbm, in_hbm],
        out_specs=(on_chip, on_chip),
        scratch_shapes=[
            pltpu.SMEM(alignment.shape, jnp.int32),
            pltpu.VMEM(diffusion_mask.shape, jnp.int32),
            pltpu.VMEM((2, BLK, width), jnp.bfloat16),
            pltpu.VMEM((3, 2, BLK, width), jnp.bfloat16),
            pltpu.VMEM((BLK, LANES), jnp.float32),
            pltpu.VMEM((3, chunks, 2 * heads, BLK), jnp.float32),
            pltpu.VMEM((3, chunks, 2 * heads, BLK), jnp.float32),
            pltpu.SemaphoreType.DMA((2,)),
            pltpu.SemaphoreType.DMA((2, 2, width // OWN)),
            pltpu.SemaphoreType.DMA((2, 2, width // OWN)),
            pltpu.SemaphoreType.DMA((chunks,)),
            pltpu.SemaphoreType.DMA((chunks,)),
            pltpu.SemaphoreType.DMA((3, chunks)),
            pltpu.SemaphoreType.DMA((3, chunks)),
            pltpu.SemaphoreType.DMA((2,)),
        ],
        compiler_params=pltpu.CompilerParams(
            collective_id=0, has_side_effects=True, vmem_limit_bytes=24 << 20
        ),
    )(
        kept(alignment),
        source_length,
        target_length,
        kept(diffusion_mask),
        kept(first_rows),
        kept(second_rows),
    )
    return pl.pallas_call(
        store,
        out_shape=(shape, shape),
        in_specs=[on_chip, on_chip],
        out_specs=(anywhere, anywhere),
        scratch_shapes=[pltpu.SemaphoreType.DMA((2,))],
        compiler_params=pltpu.CompilerParams(vmem_limit_bytes=4 << 20),
    )(*made)


def solution(mesh):
    placed = (
        P("section", "sample", "seq", None),
        P("section", "sample", "seq", None),
        P("sample", "seq", None),
        P("sample", "seq"),
        P("sample"),
        P("sample"),
    )
    return jax.shard_map(
        on_device,
        mesh=mesh,
        in_specs=placed,
        out_specs=(P("section", "sample", "seq", None), P("section", "sample", "seq", None)),
        check_vma=False,
    )
```

```python
import functools

import jax
import jax.numpy as jnp
from jax import lax
from jax.experimental import pallas as pl
from jax.experimental.pallas import tpu as pltpu
from jax.sharding import PartitionSpec as P

HDIM = 64
BLK = 128
CW = 256
OWN = 128
AHEAD = 4
LANES = 128
SCALE = HDIM**-0.5
LOG2E = 1.4426950408889634
BIG = 1e30
MESH = pl.DeviceIdType.MESH
NT = (((1,), (1,)), ((), ()))
NN = (((1,), (0,)), ((), ()))


def dot(a, b, dims):
    return lax.dot_general(a, b, dims, preferred_element_type=jnp.float32)


def kernel(
    count,
    align_in,
    source_len,
    target_len,
    mask_in,
    first,
    second,
    grad_first,
    grad_second,
    align,
    mask,
    own,
    recv,
    keep_rows,
    stat_out,
    stat_in,
    own_sem,
    send_sem,
    recv_sem,
    relay_send,
    relay_recv,
    stat_send,
    stat_recv,
    small_sem,
):
    width = first.shape[-1]
    chunks = width // CW
    heads = CW // HDIM
    section = lax.axis_index("section")
    seq = lax.axis_index("seq")
    step = 2 * section - 1
    ahead = lax.rem(seq + step + count, count)
    behind = lax.rem(seq - step + count, count)
    partner = {"section": 1 - section, "seq": seq}
    side = {"section": 1 - section, "seq": ahead}
    far = {"section": 1 - section, "seq": behind}
    relay_to = {"section": section, "seq": ahead}
    relay_from = {"section": section, "seq": behind}

    inputs = (first, second)

    def columns(c):
        return pl.ds(pl.multiple_of(c * CW, CW), CW)

    def own_copy(arr):
        return pltpu.make_async_copy(inputs[arr].at[0, 0], own.at[arr], own_sem.at[arr])

    def block_copy(slot, arr, g):
        part = pl.ds(pl.multiple_of(g * OWN, OWN), OWN)
        return pltpu.make_async_remote_copy(
            src_ref=inputs[arr].at[0, 0, :, part],
            dst_ref=recv.at[slot, arr, :, part],
            send_sem=send_sem.at[slot, arr, g],
            recv_sem=recv_sem.at[slot, arr, g],
            device_id=(partner, side)[slot],
            device_id_type=MESH,
        )

    def relay_copy(c):
        return pltpu.make_async_remote_copy(
            src_ref=recv.at[0, :, :, columns(c)],
            dst_ref=recv.at[2, :, :, columns(c)],
            send_sem=relay_send.at[c],
            recv_sem=relay_recv.at[c],
            device_id=relay_to,
            device_id_type=MESH,
        )

    def stat_copy(slot, c):
        return pltpu.make_async_remote_copy(
            src_ref=stat_out.at[slot, c],
            dst_ref=stat_in.at[slot, c],
            send_sem=stat_send.at[slot, c],
            recv_sem=stat_recv.at[slot, c],
            device_id=(partner, side, far)[slot],
            device_id_type=MESH,
        )

    has_ahead = (seq + step >= 0) & (seq + step < count)
    has_behind = (seq - step >= 0) & (seq - step < count)

    barrier = pltpu.get_barrier_semaphore()

    def greet(*peers):
        for peer in peers:
            pl.semaphore_signal(barrier, inc=1, device_id=peer, device_id_type=MESH)

    greet(partner)
    pl.when(has_ahead)(lambda: greet(side))

    small = [
        pltpu.make_async_copy(src, dst, small_sem.at[i])
        for i, (src, dst) in enumerate(
            ((align_in, align), (mask_in, mask))
        )
    ]
    for copy in small:
        copy.start()
    for arr in range(2):
        own_copy(arr).start()
    pl.semaphore_wait(barrier, 1 + has_ahead.astype(jnp.int32))

    def for_slots(slots, act):
        conditions = (None, has_ahead, has_behind)
        for slot in slots:
            if slot == 0:
                act(slot)
            else:
                pl.when(conditions[slot])(functools.partial(act, slot))

    def send_own(g, carry):
        def act(slot):
            for arr in range(2):
                block_copy(slot, arr, g).start()

        for_slots((0, 1), act)
        return carry

    lax.fori_loop(0, width // OWN, send_own, 0)

    def relay(c):
        for part in range(CW // OWN):
            for arr in range(2):
                block_copy(0, arr, c * (CW // OWN) + part).wait_recv()
        pl.when(has_ahead)(lambda: relay_copy(c).start())

    groups = width // OWN
    waited = jnp.where(has_behind, groups - 2, groups)

    def wait_ahead(g, carry):
        for arr in range(2):
            block_copy(1, arr, g).wait_recv()
        return carry

    pl.when(has_ahead)(lambda: lax.fori_loop(0, waited, wait_ahead, None))

    def relay_some(c, carry):
        relay(c)
        return carry

    lax.fori_loop(0, jnp.where(section == 1, min(AHEAD, chunks), chunks), relay_some, 0)

    for copy in small:
        copy.wait()
    for arr in range(2):
        own_copy(arr).wait()

    lane = lax.broadcasted_iota(jnp.int32, (1, LANES), 1)
    row = lax.broadcasted_iota(jnp.int32, (BLK, LANES), 0)
    low_half = lane < HDIM
    half_mask = (
        low_half.astype(jnp.float32).astype(jnp.bfloat16),
        (1.0 - low_half.astype(jnp.float32)).astype(jnp.bfloat16),
    )

    def stacked(block):
        return jnp.concatenate([block * half_mask[0], block * half_mask[1]], axis=0)

    limit = target_len[0]
    source_end = source_len[0]

    @pl.when(section == 1)
    def _():
        missing = 2 * seq - align[0, 0, 0] - align[0, 0, 1]
        lower_missing = missing == -1
        upper_missing = missing == 1
        first_block = jnp.where(lower_missing, seq, seq - 1)
        second_block = jnp.where(upper_missing, seq, seq + 1)
        key_pos = lane - source_end
        key_pos = jnp.concatenate([first_block * BLK + key_pos, second_block * BLK + key_pos], axis=1)
        key_valid = key_pos < 0
        live_lane = (seq * BLK + lane < limit).astype(jnp.float32)
        keep_lane = live_lane * (mask[...] == 1).astype(jnp.float32)
        keep_rows[...] = jnp.broadcast_to(keep_lane, (BLK, LANES)).T
        listed = tuple(
            jnp.where(missing == offset, jnp.float32(0.0), jnp.float32(1.0)) for offset in (0, 1, -1)
        )
        stat_lane = lax.broadcasted_iota(jnp.int32, (BLK, LANES), 1)
        stat_row = lax.broadcasted_iota(jnp.int32, (2 * heads, LANES), 0)

        def body(c, carry):
            pl.when((c == chunks - 1) & has_ahead)(lambda: lax.fori_loop(waited, groups, wait_ahead, None))
            pl.when(has_behind)(lambda: relay_copy(c).wait_recv())
            live = seq * BLK + jnp.concatenate([row, row], axis=0) < limit
            stats = jnp.zeros((BLK, LANES), jnp.float32)
            saved = []
            for pair in range(CW // LANES):
                cols = pl.ds(pl.multiple_of(c * CW + pair * LANES, LANES), LANES)
                query = own[0, :, cols]
                cot = own[1, :, cols]
                kv = []
                for arr in range(2):
                    middle = recv[0, arr, :, cols]
                    lower = lax.select(lower_missing, middle, recv[2, arr, :, cols])
                    upper = lax.select(upper_missing, middle, recv[1, arr, :, cols])
                    kv.append(jnp.concatenate([lower, upper], axis=0))
                keys, values = kv
                cots = stacked(cot)
                scores = dot(stacked(query), keys, NT) * (SCALE * LOG2E)
                scores = jnp.where(key_valid, scores, -BIG)
                peak = jnp.max(scores, axis=-1, keepdims=True)
                expo = jnp.exp2(scores - peak)
                total = jnp.sum(expo, axis=-1, keepdims=True)
                probs = expo * (1.0 / total)
                attended = dot(probs.astype(jnp.bfloat16), values, NN)
                out_low = jnp.where(live, attended, 0.0).astype(jnp.bfloat16).astype(jnp.float32)
                delta = jnp.sum(cots.astype(jnp.float32) * out_low, axis=-1, keepdims=True)
                lse = peak + jnp.log(total) * LOG2E
                for half in range(2):
                    head = 2 * pair + half
                    rows = slice(half * BLK, (half + 1) * BLK)
                    stats = jnp.where(stat_lane == head, lse[rows], stats)
                    stats = jnp.where(stat_lane == heads + head, delta[rows], stats)
                saved.append((cots, keys, values, probs, delta))
                halves = out_low[:BLK], out_low[BLK:]
                grad_second[0, 0, :, cols] = jnp.where(low_half, halves[0], halves[1]).astype(jnp.bfloat16)
            stats = stats.T[: 2 * heads]
            for slot in range(3):
                kept = keep_lane * listed[slot]
                stat_out[slot, c] = jnp.where((stat_row >= heads) | (kept == 1.0), stats, BIG)
            for_slots((2, 1, 0), lambda slot: stat_copy(slot, c).start())
            pl.when(c + AHEAD < chunks)(lambda: relay(c + AHEAD))

            for pair in range(CW // LANES):
                cols = pl.ds(pl.multiple_of(c * CW + pair * LANES, LANES), LANES)
                cots, keys, values, probs, delta = saved[pair]
                dprob = dot(cots, values, NT)
                dscore = (probs * (dprob - delta)).astype(jnp.bfloat16)
                queries_grad = dot(dscore, keys, NN)
                halves = queries_grad[:BLK], queries_grad[BLK:]
                dquery = jnp.where(low_half, halves[0], halves[1]) * SCALE
                dquery = jnp.where(keep_rows[...] == 1.0, dquery, 0.0)
                grad_first[0, 0, :, cols] = dquery.astype(jnp.bfloat16)
            return carry

        lax.fori_loop(0, chunks, body, 0)

        def drain(c, carry):
            for_slots(range(3), lambda slot: stat_copy(slot, c).wait_send())
            return carry

        lax.fori_loop(0, chunks, drain, 0)

    @pl.when(section == 0)
    def _():
        def absent(slot):
            recv[slot] = jnp.zeros_like(recv[slot])
            stat_in[slot] = jnp.full_like(stat_in[slot], BIG)

        pl.when(jnp.logical_not(has_ahead))(lambda: absent(1))
        pl.when(jnp.logical_not(has_behind))(lambda: absent(2))

        def body(c, carry):
            pl.when((c == chunks - 1) & has_ahead)(lambda: lax.fori_loop(waited, groups, wait_ahead, None))
            pl.when(has_behind)(lambda: relay_copy(c).wait_recv())
            for_slots(range(3), lambda slot: stat_copy(slot, c).wait_recv())
            valid = seq * BLK + row < source_end
            stats = jnp.concatenate([stat_in[slot, c] for slot in range(3)], axis=1)
            for pair in range(CW // LANES):
                cols = pl.ds(pl.multiple_of(c * CW + pair * LANES, LANES), LANES)
                queries = recv[:, 0, :, cols].reshape(3 * BLK, LANES)
                cots = recv[:, 1, :, cols].reshape(3 * BLK, LANES)

                def per_key(base):
                    rows = [stats[base + 2 * pair + half : base + 2 * pair + half + 1] for half in range(2)]
                    return jnp.concatenate([jnp.broadcast_to(line, (BLK, 3 * BLK)) for line in rows], axis=0)

                scores = dot(stacked(own[0, :, cols]), queries, NT) * (SCALE * LOG2E)
                probs = jnp.exp2(scores - per_key(0))
                dprob = dot(stacked(own[1, :, cols]), cots, NT)
                dscore = probs * (dprob - per_key(heads))
                dvalue = dot(probs.astype(jnp.bfloat16), cots, NN)
                dkey = dot(dscore.astype(jnp.bfloat16), queries, NN)
                dkey = jnp.where(low_half, dkey[:BLK], dkey[BLK:]) * SCALE
                dvalue = jnp.where(low_half, dvalue[:BLK], dvalue[BLK:])
                grad_first[0, 0, :, cols] = jnp.where(valid, dkey, 0.0).astype(jnp.bfloat16)
                grad_second[0, 0, :, cols] = jnp.where(valid, dvalue, 0.0).astype(jnp.bfloat16)
            return carry

        lax.fori_loop(0, chunks, body, 0)

    def drain_own(g, carry):
        def act(slot):
            for arr in range(2):
                block_copy(slot, arr, g).wait_send()

        for_slots((0, 1), act)
        return carry

    def drain_relay(c, carry):
        relay_copy(c).wait_send()
        return carry

    lax.fori_loop(0, groups, drain_own, 0)
    pl.when(has_ahead)(lambda: lax.fori_loop(0, chunks, drain_relay, None))


def store(first, second, grad_first, grad_second, sems):
    copies = (
        pltpu.make_async_copy(first, grad_first, sems.at[0]),
        pltpu.make_async_copy(second, grad_second, sems.at[1]),
    )
    for copy in copies:
        copy.start()
    for copy in copies:
        copy.wait()


def on_device(first_rows, second_rows, alignment, diffusion_mask, source_length, target_length):
    count = lax.axis_size("seq")
    width = first_rows.shape[3]
    chunks = width // CW
    heads = CW // HDIM
    shape = jax.ShapeDtypeStruct(first_rows.shape, jnp.bfloat16)
    anywhere = pl.BlockSpec(memory_space=pl.ANY)
    on_chip = pl.BlockSpec(memory_space=pltpu.VMEM)
    in_hbm = pl.BlockSpec(memory_space=pltpu.HBM)
    scalars = pl.BlockSpec(memory_space=pltpu.SMEM)

    def kept(array):
        return pltpu.with_memory_space_constraint(array, pltpu.HBM)

    made = pl.pallas_call(
        functools.partial(kernel, count),
        out_shape=(shape, shape),
        in_specs=[in_hbm, scalars, scalars, in_hbm, in_hbm, in_hbm],
        out_specs=(on_chip, on_chip),
        scratch_shapes=[
            pltpu.SMEM(alignment.shape, jnp.int32),
            pltpu.VMEM(diffusion_mask.shape, jnp.int32),
            pltpu.VMEM((2, BLK, width), jnp.bfloat16),
            pltpu.VMEM((3, 2, BLK, width), jnp.bfloat16),
            pltpu.VMEM((BLK, LANES), jnp.float32),
            pltpu.VMEM((3, chunks, 2 * heads, BLK), jnp.float32),
            pltpu.VMEM((3, chunks, 2 * heads, BLK), jnp.float32),
            pltpu.SemaphoreType.DMA((2,)),
            pltpu.SemaphoreType.DMA((2, 2, width // OWN)),
            pltpu.SemaphoreType.DMA((2, 2, width // OWN)),
            pltpu.SemaphoreType.DMA((chunks,)),
            pltpu.SemaphoreType.DMA((chunks,)),
            pltpu.SemaphoreType.DMA((3, chunks)),
            pltpu.SemaphoreType.DMA((3, chunks)),
            pltpu.SemaphoreType.DMA((2,)),
        ],
        compiler_params=pltpu.CompilerParams(
            collective_id=0, has_side_effects=True, vmem_limit_bytes=24 << 20
        ),
    )(
        kept(alignment),
        source_length,
        target_length,
        kept(diffusion_mask),
        kept(first_rows),
        kept(second_rows),
    )
    return pl.pallas_call(
        store,
        out_shape=(shape, shape),
        in_specs=[on_chip, on_chip],
        out_specs=(anywhere, anywhere),
        scratch_shapes=[pltpu.SemaphoreType.DMA((2,))],
        compiler_params=pltpu.CompilerParams(vmem_limit_bytes=4 << 20),
    )(*made)


def solution(mesh):
    placed = (
        P("section", "sample", "seq", None),
        P("section", "sample", "seq", None),
        P("sample", "seq", None),
        P("sample", "seq"),
        P("sample"),
        P("sample"),
    )
    return jax.shard_map(
        on_device,
        mesh=mesh,
        in_specs=placed,
        out_specs=(P("section", "sample", "seq", None), P("section", "sample", "seq", None)),
        check_vma=False,
    )
```

```python
import functools

import jax
import jax.numpy as jnp
from jax import lax
from jax.experimental import pallas as pl
from jax.experimental.pallas import tpu as pltpu
from jax.sharding import PartitionSpec as P

HDIM = 64
BLK = 128
CW = 256
OWN = 128
AHEAD = 4
LANES = 128
SCALE = HDIM**-0.5
LOG2E = 1.4426950408889634
BIG = 1e30
MESH = pl.DeviceIdType.MESH
NT = (((1,), (1,)), ((), ()))
NN = (((1,), (0,)), ((), ()))


def dot(a, b, dims):
    return lax.dot_general(a, b, dims, preferred_element_type=jnp.float32)


def kernel(
    count,
    align_in,
    source_len,
    target_len,
    mask_in,
    first,
    second,
    grad_first,
    grad_second,
    align,
    mask,
    own,
    recv,
    keep_rows,
    stat_out,
    stat_in,
    own_sem,
    send_sem,
    recv_sem,
    relay_send,
    relay_recv,
    stat_send,
    stat_recv,
    small_sem,
):
    width = first.shape[-1]
    whole = width // CW - 1
    chunks = whole + CW // LANES
    heads = CW // HDIM
    section = lax.axis_index("section")
    seq = lax.axis_index("seq")
    step = 2 * section - 1
    ahead = lax.rem(seq + step + count, count)
    behind = lax.rem(seq - step + count, count)
    partner = {"section": 1 - section, "seq": seq}
    side = {"section": 1 - section, "seq": ahead}
    far = {"section": 1 - section, "seq": behind}
    relay_to = {"section": section, "seq": ahead}
    relay_from = {"section": section, "seq": behind}

    inputs = (first, second)

    def start_of(c, size):
        return c * CW if size == CW else whole * CW + (c - whole) * LANES

    def columns(c, size):
        return pl.ds(pl.multiple_of(start_of(c, size), size), size)

    def for_sizes(act):
        def loop(low, high, size):
            def body(c, carry):
                act(c, size)
                return carry

            lax.fori_loop(low, high, body, 0)

        loop(0, whole, CW)
        loop(whole, chunks, LANES)

    def own_copy(arr):
        return pltpu.make_async_copy(inputs[arr].at[0, 0], own.at[arr], own_sem.at[arr])

    def block_copy(slot, arr, g):
        part = pl.ds(pl.multiple_of(g * OWN, OWN), OWN)
        return pltpu.make_async_remote_copy(
            src_ref=inputs[arr].at[0, 0, :, part],
            dst_ref=recv.at[slot, arr, :, part],
            send_sem=send_sem.at[slot, arr, g],
            recv_sem=recv_sem.at[slot, arr, g],
            device_id=(partner, side)[slot],
            device_id_type=MESH,
        )

    def relay_copy(c, size):
        return pltpu.make_async_remote_copy(
            src_ref=recv.at[0, :, :, columns(c, size)],
            dst_ref=recv.at[2, :, :, columns(c, size)],
            send_sem=relay_send.at[c],
            recv_sem=relay_recv.at[c],
            device_id=relay_to,
            device_id_type=MESH,
        )

    def stat_copy(slot, c):
        return pltpu.make_async_remote_copy(
            src_ref=stat_out.at[slot, c],
            dst_ref=stat_in.at[slot, c],
            send_sem=stat_send.at[slot, c],
            recv_sem=stat_recv.at[slot, c],
            device_id=(partner, side, far)[slot],
            device_id_type=MESH,
        )

    has_ahead = (seq + step >= 0) & (seq + step < count)
    has_behind = (seq - step >= 0) & (seq - step < count)

    barrier = pltpu.get_barrier_semaphore()

    def greet(*peers):
        for peer in peers:
            pl.semaphore_signal(barrier, inc=1, device_id=peer, device_id_type=MESH)

    greet(partner)
    pl.when(has_ahead)(lambda: greet(side))

    small = [
        pltpu.make_async_copy(src, dst, small_sem.at[i])
        for i, (src, dst) in enumerate(
            ((align_in, align), (mask_in, mask))
        )
    ]
    for copy in small:
        copy.start()
    for arr in range(2):
        own_copy(arr).start()
    pl.semaphore_wait(barrier, 1 + has_ahead.astype(jnp.int32))

    def for_slots(slots, act):
        conditions = (None, has_ahead, has_behind)
        for slot in slots:
            if slot == 0:
                act(slot)
            else:
                pl.when(conditions[slot])(functools.partial(act, slot))

    def send_own(g, carry):
        def act(slot):
            for arr in range(2):
                block_copy(slot, arr, g).start()

        for_slots((0, 1), act)
        return carry

    lax.fori_loop(0, width // OWN, send_own, 0)

    def relay(c, size):
        for part in range(size // OWN):
            for arr in range(2):
                block_copy(0, arr, start_of(c, size) // OWN + part).wait_recv()
        pl.when(has_ahead)(lambda: relay_copy(c, size).start())

    def relay_rest():
        def one(c, carry):
            relay(c, LANES)
            return carry

        lax.fori_loop(whole, chunks, one, 0)

    groups = width // OWN
    waited = jnp.where(has_behind, groups - 2, groups)

    def wait_ahead(g, carry):
        for arr in range(2):
            block_copy(1, arr, g).wait_recv()
        return carry

    pl.when(has_ahead)(lambda: lax.fori_loop(0, waited, wait_ahead, None))

    def relay_some(c, carry):
        relay(c, CW)
        return carry

    under_way = min(AHEAD, whole)
    lax.fori_loop(0, jnp.where(section == 1, under_way, whole), relay_some, 0)
    pl.when(section == 0)(relay_rest)

    for copy in small:
        copy.wait()
    for arr in range(2):
        own_copy(arr).wait()

    lane = lax.broadcasted_iota(jnp.int32, (1, LANES), 1)
    row = lax.broadcasted_iota(jnp.int32, (BLK, LANES), 0)
    low_half = lane < HDIM
    half_mask = (
        low_half.astype(jnp.float32).astype(jnp.bfloat16),
        (1.0 - low_half.astype(jnp.float32)).astype(jnp.bfloat16),
    )

    def stacked(block):
        return jnp.concatenate([block * half_mask[0], block * half_mask[1]], axis=0)

    limit = target_len[0]
    source_end = source_len[0]

    @pl.when(section == 1)
    def _():
        missing = 2 * seq - align[0, 0, 0] - align[0, 0, 1]
        lower_missing = missing == -1
        upper_missing = missing == 1
        first_block = jnp.where(lower_missing, seq, seq - 1)
        second_block = jnp.where(upper_missing, seq, seq + 1)
        key_pos = lane - source_end
        key_pos = jnp.concatenate([first_block * BLK + key_pos, second_block * BLK + key_pos], axis=1)
        key_valid = key_pos < 0
        live_lane = (seq * BLK + lane < limit).astype(jnp.float32)
        keep_lane = live_lane * (mask[...] == 1).astype(jnp.float32)
        keep_rows[...] = jnp.broadcast_to(keep_lane, (BLK, LANES)).T
        listed = tuple(
            jnp.where(missing == offset, jnp.float32(0.0), jnp.float32(1.0)) for offset in (0, 1, -1)
        )
        stat_lane = lax.broadcasted_iota(jnp.int32, (BLK, LANES), 1)
        stat_row = lax.broadcasted_iota(jnp.int32, (2 * heads, LANES), 0)

        def step_of(c, size):
            pl.when((c == whole) & has_ahead)(lambda: lax.fori_loop(waited, groups, wait_ahead, None))
            pl.when(has_behind)(lambda: relay_copy(c, size).wait_recv())
            live = seq * BLK + jnp.concatenate([row, row], axis=0) < limit
            stats = jnp.zeros((BLK, LANES), jnp.float32)
            saved = []
            for pair in range(size // LANES):
                cols = pl.ds(pl.multiple_of(start_of(c, size) + pair * LANES, LANES), LANES)
                query = own[0, :, cols]
                cot = own[1, :, cols]
                kv = []
                for arr in range(2):
                    middle = recv[0, arr, :, cols]
                    lower = lax.select(lower_missing, middle, recv[2, arr, :, cols])
                    upper = lax.select(upper_missing, middle, recv[1, arr, :, cols])
                    kv.append(jnp.concatenate([lower, upper], axis=0))
                keys, values = kv
                cots = stacked(cot)
                scores = dot(stacked(query), keys, NT) * (SCALE * LOG2E)
                scores = jnp.where(key_valid, scores, -BIG)
                peak = jnp.max(scores, axis=-1, keepdims=True)
                expo = jnp.exp2(scores - peak)
                total = jnp.sum(expo, axis=-1, keepdims=True)
                probs = expo * (1.0 / total)
                attended = dot(probs.astype(jnp.bfloat16), values, NN)
                out_low = jnp.where(live, attended, 0.0).astype(jnp.bfloat16).astype(jnp.float32)
                delta = jnp.sum(cots.astype(jnp.float32) * out_low, axis=-1, keepdims=True)
                lse = peak + jnp.log(total) * LOG2E
                for half in range(2):
                    head = 2 * pair + half
                    rows = slice(half * BLK, (half + 1) * BLK)
                    stats = jnp.where(stat_lane == head, lse[rows], stats)
                    stats = jnp.where(stat_lane == heads + head, delta[rows], stats)
                saved.append((cots, keys, values, probs, delta))
                halves = out_low[:BLK], out_low[BLK:]
                grad_second[0, 0, :, cols] = jnp.where(low_half, halves[0], halves[1]).astype(jnp.bfloat16)
            stats = stats.T[: 2 * heads]
            for slot in range(3):
                kept = keep_lane * listed[slot]
                stat_out[slot, c] = jnp.where((stat_row >= heads) | (kept == 1.0), stats, BIG)
            for_slots((2, 1, 0), lambda slot: stat_copy(slot, c).start())
            if size == CW:
                pl.when(c + under_way < whole)(lambda: relay(c + under_way, CW))
                pl.when(c + under_way == whole)(relay_rest)

            for pair in range(size // LANES):
                cols = pl.ds(pl.multiple_of(start_of(c, size) + pair * LANES, LANES), LANES)
                cots, keys, values, probs, delta = saved[pair]
                dprob = dot(cots, values, NT)
                dscore = (probs * (dprob - delta)).astype(jnp.bfloat16)
                queries_grad = dot(dscore, keys, NN)
                halves = queries_grad[:BLK], queries_grad[BLK:]
                dquery = jnp.where(low_half, halves[0], halves[1]) * SCALE
                dquery = jnp.where(keep_rows[...] == 1.0, dquery, 0.0)
                grad_first[0, 0, :, cols] = dquery.astype(jnp.bfloat16)

        for_sizes(step_of)

        def drain(c, carry):
            for_slots(range(3), lambda slot: stat_copy(slot, c).wait_send())
            return carry

        lax.fori_loop(0, chunks, drain, 0)

    @pl.when(section == 0)
    def _():
        def absent(slot):
            recv[slot] = jnp.zeros_like(recv[slot])
            stat_in[slot] = jnp.full_like(stat_in[slot], BIG)

        pl.when(jnp.logical_not(has_ahead))(lambda: absent(1))
        pl.when(jnp.logical_not(has_behind))(lambda: absent(2))

        def step_of(c, size):
            pl.when((c == whole) & has_ahead)(lambda: lax.fori_loop(waited, groups, wait_ahead, None))
            pl.when(has_behind)(lambda: relay_copy(c, size).wait_recv())
            for_slots(range(3), lambda slot: stat_copy(slot, c).wait_recv())
            valid = seq * BLK + row < source_end
            stats = jnp.concatenate([stat_in[slot, c] for slot in range(3)], axis=1)
            for pair in range(size // LANES):
                cols = pl.ds(pl.multiple_of(start_of(c, size) + pair * LANES, LANES), LANES)
                queries = recv[:, 0, :, cols].reshape(3 * BLK, LANES)
                cots = recv[:, 1, :, cols].reshape(3 * BLK, LANES)

                def per_key(base):
                    rows = [stats[base + 2 * pair + half : base + 2 * pair + half + 1] for half in range(2)]
                    return jnp.concatenate([jnp.broadcast_to(line, (BLK, 3 * BLK)) for line in rows], axis=0)

                scores = dot(stacked(own[0, :, cols]), queries, NT) * (SCALE * LOG2E)
                probs = jnp.exp2(scores - per_key(0))
                dprob = dot(stacked(own[1, :, cols]), cots, NT)
                dscore = probs * (dprob - per_key(heads))
                dvalue = dot(probs.astype(jnp.bfloat16), cots, NN)
                dkey = dot(dscore.astype(jnp.bfloat16), queries, NN)
                dkey = jnp.where(low_half, dkey[:BLK], dkey[BLK:]) * SCALE
                dvalue = jnp.where(low_half, dvalue[:BLK], dvalue[BLK:])
                grad_first[0, 0, :, cols] = jnp.where(valid, dkey, 0.0).astype(jnp.bfloat16)
                grad_second[0, 0, :, cols] = jnp.where(valid, dvalue, 0.0).astype(jnp.bfloat16)

        for_sizes(step_of)

    def drain_own(g, carry):
        def act(slot):
            for arr in range(2):
                block_copy(slot, arr, g).wait_send()

        for_slots((0, 1), act)
        return carry

    def drain_relay(c, size):
        relay_copy(c, size).wait_send()

    lax.fori_loop(0, groups, drain_own, 0)
    pl.when(has_ahead)(lambda: for_sizes(drain_relay))


def store(first, second, grad_first, grad_second, sems):
    copies = (
        pltpu.make_async_copy(first, grad_first, sems.at[0]),
        pltpu.make_async_copy(second, grad_second, sems.at[1]),
    )
    for copy in copies:
        copy.start()
    for copy in copies:
        copy.wait()


def on_device(first_rows, second_rows, alignment, diffusion_mask, source_length, target_length):
    count = lax.axis_size("seq")
    width = first_rows.shape[3]
    chunks = width // CW - 1 + CW // LANES
    heads = CW // HDIM
    shape = jax.ShapeDtypeStruct(first_rows.shape, jnp.bfloat16)
    anywhere = pl.BlockSpec(memory_space=pl.ANY)
    on_chip = pl.BlockSpec(memory_space=pltpu.VMEM)
    in_hbm = pl.BlockSpec(memory_space=pltpu.HBM)
    scalars = pl.BlockSpec(memory_space=pltpu.SMEM)

    def kept(array):
        return pltpu.with_memory_space_constraint(array, pltpu.HBM)

    made = pl.pallas_call(
        functools.partial(kernel, count),
        out_shape=(shape, shape),
        in_specs=[in_hbm, scalars, scalars, in_hbm, in_hbm, in_hbm],
        out_specs=(on_chip, on_chip),
        scratch_shapes=[
            pltpu.SMEM(alignment.shape, jnp.int32),
            pltpu.VMEM(diffusion_mask.shape, jnp.int32),
            pltpu.VMEM((2, BLK, width), jnp.bfloat16),
            pltpu.VMEM((3, 2, BLK, width), jnp.bfloat16),
            pltpu.VMEM((BLK, LANES), jnp.float32),
            pltpu.VMEM((3, chunks, 2 * heads, BLK), jnp.float32),
            pltpu.VMEM((3, chunks, 2 * heads, BLK), jnp.float32),
            pltpu.SemaphoreType.DMA((2,)),
            pltpu.SemaphoreType.DMA((2, 2, width // OWN)),
            pltpu.SemaphoreType.DMA((2, 2, width // OWN)),
            pltpu.SemaphoreType.DMA((chunks,)),
            pltpu.SemaphoreType.DMA((chunks,)),
            pltpu.SemaphoreType.DMA((3, chunks)),
            pltpu.SemaphoreType.DMA((3, chunks)),
            pltpu.SemaphoreType.DMA((2,)),
        ],
        compiler_params=pltpu.CompilerParams(
            collective_id=0, has_side_effects=True, vmem_limit_bytes=24 << 20,
        ),
    )(
        kept(alignment),
        source_length,
        target_length,
        kept(diffusion_mask),
        kept(first_rows),
        kept(second_rows),
    )
    return pl.pallas_call(
        store,
        out_shape=(shape, shape),
        in_specs=[on_chip, on_chip],
        out_specs=(anywhere, anywhere),
        scratch_shapes=[pltpu.SemaphoreType.DMA((2,))],
        compiler_params=pltpu.CompilerParams(vmem_limit_bytes=4 << 20),
    )(*made)


def solution(mesh):
    placed = (
        P("section", "sample", "seq", None),
        P("section", "sample", "seq", None),
        P("sample", "seq", None),
        P("sample", "seq"),
        P("sample"),
        P("sample"),
    )
    return jax.shard_map(
        on_device,
        mesh=mesh,
        in_specs=placed,
        out_specs=(P("section", "sample", "seq", None), P("section", "sample", "seq", None)),
        check_vma=False,
    )
```

```python
import functools

import jax
import jax.numpy as jnp
from jax import lax
from jax.experimental import pallas as pl
from jax.experimental.pallas import tpu as pltpu
from jax.sharding import PartitionSpec as P

HDIM = 64
BLK = 128
CW = 256
OWN = 128
AHEAD = 4
LANES = 128
TAIL = 2
SCALE = HDIM**-0.5
LOG2E = 1.4426950408889634
BIG = 1e30
MESH = pl.DeviceIdType.MESH
NT = (((1,), (1,)), ((), ()))
NN = (((1,), (0,)), ((), ()))


def dot(a, b, dims):
    return lax.dot_general(a, b, dims, preferred_element_type=jnp.float32)


def kernel(
    count,
    align_in,
    source_len,
    target_len,
    mask_in,
    first,
    second,
    grad_first,
    grad_second,
    align,
    mask,
    own,
    recv,
    keep_rows,
    stat_out,
    stat_in,
    own_sem,
    send_sem,
    recv_sem,
    relay_send,
    relay_recv,
    stat_send,
    stat_recv,
    small_sem,
):
    width = first.shape[-1]
    whole = max(width // CW - TAIL, 1)
    chunks = whole + (width // CW - whole) * (CW // LANES)
    heads = CW // HDIM
    section = lax.axis_index("section")
    seq = lax.axis_index("seq")
    step = 2 * section - 1
    ahead = lax.rem(seq + step + count, count)
    behind = lax.rem(seq - step + count, count)
    partner = {"section": 1 - section, "seq": seq}
    side = {"section": 1 - section, "seq": ahead}
    far = {"section": 1 - section, "seq": behind}
    relay_to = {"section": section, "seq": ahead}
    relay_from = {"section": section, "seq": behind}

    inputs = (first, second)

    def start_of(c, size):
        return c * CW if size == CW else whole * CW + (c - whole) * LANES

    def columns(c, size):
        return pl.ds(pl.multiple_of(start_of(c, size), size), size)

    def for_sizes(act):
        def loop(low, high, size):
            def body(c, carry):
                act(c, size)
                return carry

            lax.fori_loop(low, high, body, 0)

        loop(0, whole, CW)
        loop(whole, chunks, LANES)

    def own_copy(arr):
        return pltpu.make_async_copy(inputs[arr].at[0, 0], own.at[arr], own_sem.at[arr])

    def block_copy(slot, arr, g):
        part = pl.ds(pl.multiple_of(g * OWN, OWN), OWN)
        return pltpu.make_async_remote_copy(
            src_ref=inputs[arr].at[0, 0, :, part],
            dst_ref=recv.at[slot, arr, :, part],
            send_sem=send_sem.at[slot, arr, g],
            recv_sem=recv_sem.at[slot, arr, g],
            device_id=(partner, side)[slot],
            device_id_type=MESH,
        )

    def relay_copy(c, size):
        return pltpu.make_async_remote_copy(
            src_ref=recv.at[0, :, :, columns(c, size)],
            dst_ref=recv.at[2, :, :, columns(c, size)],
            send_sem=relay_send.at[c],
            recv_sem=relay_recv.at[c],
            device_id=relay_to,
            device_id_type=MESH,
        )

    def stat_copy(slot, c):
        return pltpu.make_async_remote_copy(
            src_ref=stat_out.at[slot, c],
            dst_ref=stat_in.at[slot, c],
            send_sem=stat_send.at[slot, c],
            recv_sem=stat_recv.at[slot, c],
            device_id=(partner, side, far)[slot],
            device_id_type=MESH,
        )

    has_ahead = (seq + step >= 0) & (seq + step < count)
    has_behind = (seq - step >= 0) & (seq - step < count)

    barrier = pltpu.get_barrier_semaphore()

    def greet(*peers):
        for peer in peers:
            pl.semaphore_signal(barrier, inc=1, device_id=peer, device_id_type=MESH)

    greet(partner)
    pl.when(has_ahead)(lambda: greet(side))

    small = [
        pltpu.make_async_copy(src, dst, small_sem.at[i])
        for i, (src, dst) in enumerate(
            ((align_in, align), (mask_in, mask))
        )
    ]
    for copy in small:
        copy.start()
    for arr in range(2):
        own_copy(arr).start()
    pl.semaphore_wait(barrier, 1 + has_ahead.astype(jnp.int32))

    def for_slots(slots, act):
        conditions = (None, has_ahead, has_behind)
        for slot in slots:
            if slot == 0:
                act(slot)
            else:
                pl.when(conditions[slot])(functools.partial(act, slot))

    def send_own(g, carry):
        def act(slot):
            for arr in range(2):
                block_copy(slot, arr, g).start()

        for_slots((0, 1), act)
        return carry

    lax.fori_loop(0, width // OWN, send_own, 0)

    def relay(c, size):
        for part in range(size // OWN):
            for arr in range(2):
                block_copy(0, arr, start_of(c, size) // OWN + part).wait_recv()
        pl.when(has_ahead)(lambda: relay_copy(c, size).start())

    def relay_rest():
        def one(c, carry):
            relay(c, LANES)
            return carry

        lax.fori_loop(whole, chunks, one, 0)

    groups = width // OWN
    waited = jnp.where(has_behind, groups - 2, groups)

    def wait_ahead(g, carry):
        for arr in range(2):
            block_copy(1, arr, g).wait_recv()
        return carry

    pl.when(has_ahead)(lambda: lax.fori_loop(0, waited, wait_ahead, None))

    def relay_some(c, carry):
        relay(c, CW)
        return carry

    under_way = min(AHEAD, whole)
    lax.fori_loop(0, jnp.where(section == 1, under_way, whole), relay_some, 0)
    pl.when(section == 0)(relay_rest)

    for copy in small:
        copy.wait()
    for arr in range(2):
        own_copy(arr).wait()

    lane = lax.broadcasted_iota(jnp.int32, (1, LANES), 1)
    row = lax.broadcasted_iota(jnp.int32, (BLK, LANES), 0)
    low_half = lane < HDIM
    half_mask = (
        low_half.astype(jnp.float32).astype(jnp.bfloat16),
        (1.0 - low_half.astype(jnp.float32)).astype(jnp.bfloat16),
    )

    def stacked(block):
        return jnp.concatenate([block * half_mask[0], block * half_mask[1]], axis=0)

    limit = target_len[0]
    source_end = source_len[0]

    @pl.when(section == 1)
    def _():
        missing = 2 * seq - align[0, 0, 0] - align[0, 0, 1]
        lower_missing = missing == -1
        upper_missing = missing == 1
        first_block = jnp.where(lower_missing, seq, seq - 1)
        second_block = jnp.where(upper_missing, seq, seq + 1)
        key_pos = lane - source_end
        key_pos = jnp.concatenate([first_block * BLK + key_pos, second_block * BLK + key_pos], axis=1)
        key_valid = key_pos < 0
        live_lane = (seq * BLK + lane < limit).astype(jnp.float32)
        keep_lane = live_lane * (mask[...] == 1).astype(jnp.float32)
        keep_rows[...] = jnp.broadcast_to(keep_lane, (BLK, LANES)).T
        listed = tuple(
            jnp.where(missing == offset, jnp.float32(0.0), jnp.float32(1.0)) for offset in (0, 1, -1)
        )
        stat_lane = lax.broadcasted_iota(jnp.int32, (BLK, LANES), 1)
        stat_row = lax.broadcasted_iota(jnp.int32, (2 * heads, LANES), 0)

        def step_of(c, size):
            pl.when((c == whole) & has_ahead)(lambda: lax.fori_loop(waited, groups, wait_ahead, None))
            pl.when(has_behind)(lambda: relay_copy(c, size).wait_recv())
            live = seq * BLK + jnp.concatenate([row, row], axis=0) < limit
            stats = jnp.zeros((BLK, LANES), jnp.float32)
            saved = []
            for pair in range(size // LANES):
                cols = pl.ds(pl.multiple_of(start_of(c, size) + pair * LANES, LANES), LANES)
                query = own[0, :, cols]
                cot = own[1, :, cols]
                kv = []
                for arr in range(2):
                    middle = recv[0, arr, :, cols]
                    lower = lax.select(lower_missing, middle, recv[2, arr, :, cols])
                    upper = lax.select(upper_missing, middle, recv[1, arr, :, cols])
                    kv.append(jnp.concatenate([lower, upper], axis=0))
                keys, values = kv
                cots = stacked(cot)
                scores = dot(stacked(query), keys, NT) * (SCALE * LOG2E)
                scores = jnp.where(key_valid, scores, -BIG)
                peak = jnp.max(scores, axis=-1, keepdims=True)
                expo = jnp.exp2(scores - peak)
                total = jnp.sum(expo, axis=-1, keepdims=True)
                probs = expo * (1.0 / total)
                attended = dot(probs.astype(jnp.bfloat16), values, NN)
                out_low = jnp.where(live, attended, 0.0).astype(jnp.bfloat16).astype(jnp.float32)
                delta = jnp.sum(cots.astype(jnp.float32) * out_low, axis=-1, keepdims=True)
                lse = peak + jnp.log(total) * LOG2E
                for half in range(2):
                    head = 2 * pair + half
                    rows = slice(half * BLK, (half + 1) * BLK)
                    stats = jnp.where(stat_lane == head, lse[rows], stats)
                    stats = jnp.where(stat_lane == heads + head, delta[rows], stats)
                saved.append((cots, keys, values, probs, delta))
                halves = out_low[:BLK], out_low[BLK:]
                grad_second[0, 0, :, cols] = jnp.where(low_half, halves[0], halves[1]).astype(jnp.bfloat16)
            stats = stats.T[: 2 * heads]
            for slot in range(3):
                kept = keep_lane * listed[slot]
                stat_out[slot, c] = jnp.where((stat_row >= heads) | (kept == 1.0), stats, BIG)
            for_slots((2, 1, 0), lambda slot: stat_copy(slot, c).start())
            if size == CW:
                pl.when(c + under_way < whole)(lambda: relay(c + under_way, CW))
                pl.when(c + under_way == whole)(relay_rest)

            for pair in range(size // LANES):
                cols = pl.ds(pl.multiple_of(start_of(c, size) + pair * LANES, LANES), LANES)
                cots, keys, values, probs, delta = saved[pair]
                dprob = dot(cots, values, NT)
                dscore = (probs * (dprob - delta)).astype(jnp.bfloat16)
                queries_grad = dot(dscore, keys, NN)
                halves = queries_grad[:BLK], queries_grad[BLK:]
                dquery = jnp.where(low_half, halves[0], halves[1]) * SCALE
                dquery = jnp.where(keep_rows[...] == 1.0, dquery, 0.0)
                grad_first[0, 0, :, cols] = dquery.astype(jnp.bfloat16)

        for_sizes(step_of)

        def drain(c, carry):
            for_slots(range(3), lambda slot: stat_copy(slot, c).wait_send())
            return carry

        lax.fori_loop(0, chunks, drain, 0)

    @pl.when(section == 0)
    def _():
        def absent(slot):
            recv[slot] = jnp.zeros_like(recv[slot])
            stat_in[slot] = jnp.full_like(stat_in[slot], BIG)

        pl.when(jnp.logical_not(has_ahead))(lambda: absent(1))
        pl.when(jnp.logical_not(has_behind))(lambda: absent(2))

        def step_of(c, size):
            pl.when((c == whole) & has_ahead)(lambda: lax.fori_loop(waited, groups, wait_ahead, None))
            pl.when(has_behind)(lambda: relay_copy(c, size).wait_recv())
            for_slots(range(3), lambda slot: stat_copy(slot, c).wait_recv())
            valid = seq * BLK + row < source_end
            stats = jnp.concatenate([stat_in[slot, c] for slot in range(3)], axis=1)
            for pair in range(size // LANES):
                cols = pl.ds(pl.multiple_of(start_of(c, size) + pair * LANES, LANES), LANES)
                queries = recv[:, 0, :, cols].reshape(3 * BLK, LANES)
                cots = recv[:, 1, :, cols].reshape(3 * BLK, LANES)

                def per_key(base):
                    rows = [stats[base + 2 * pair + half : base + 2 * pair + half + 1] for half in range(2)]
                    return jnp.concatenate([jnp.broadcast_to(line, (BLK, 3 * BLK)) for line in rows], axis=0)

                scores = dot(stacked(own[0, :, cols]), queries, NT) * (SCALE * LOG2E)
                probs = jnp.exp2(scores - per_key(0))
                dprob = dot(stacked(own[1, :, cols]), cots, NT)
                dscore = probs * (dprob - per_key(heads))
                dvalue = dot(probs.astype(jnp.bfloat16), cots, NN)
                dkey = dot(dscore.astype(jnp.bfloat16), queries, NN)
                dkey = jnp.where(low_half, dkey[:BLK], dkey[BLK:]) * SCALE
                dvalue = jnp.where(low_half, dvalue[:BLK], dvalue[BLK:])
                grad_first[0, 0, :, cols] = jnp.where(valid, dkey, 0.0).astype(jnp.bfloat16)
                grad_second[0, 0, :, cols] = jnp.where(valid, dvalue, 0.0).astype(jnp.bfloat16)

        for_sizes(step_of)

    def drain_own(g, carry):
        def act(slot):
            for arr in range(2):
                block_copy(slot, arr, g).wait_send()

        for_slots((0, 1), act)
        return carry

    def drain_relay(c, size):
        relay_copy(c, size).wait_send()

    lax.fori_loop(0, groups, drain_own, 0)
    pl.when(has_ahead)(lambda: for_sizes(drain_relay))


def store(first, second, grad_first, grad_second, sems):
    copies = (
        pltpu.make_async_copy(first, grad_first, sems.at[0]),
        pltpu.make_async_copy(second, grad_second, sems.at[1]),
    )
    for copy in copies:
        copy.start()
    for copy in copies:
        copy.wait()


def on_device(first_rows, second_rows, alignment, diffusion_mask, source_length, target_length):
    count = lax.axis_size("seq")
    width = first_rows.shape[3]
    whole = max(width // CW - TAIL, 1)
    chunks = whole + (width // CW - whole) * (CW // LANES)
    heads = CW // HDIM
    shape = jax.ShapeDtypeStruct(first_rows.shape, jnp.bfloat16)
    anywhere = pl.BlockSpec(memory_space=pl.ANY)
    on_chip = pl.BlockSpec(memory_space=pltpu.VMEM)
    in_hbm = pl.BlockSpec(memory_space=pltpu.HBM)
    scalars = pl.BlockSpec(memory_space=pltpu.SMEM)

    def kept(array):
        return pltpu.with_memory_space_constraint(array, pltpu.HBM)

    made = pl.pallas_call(
        functools.partial(kernel, count),
        out_shape=(shape, shape),
        in_specs=[in_hbm, scalars, scalars, in_hbm, in_hbm, in_hbm],
        out_specs=(on_chip, on_chip),
        scratch_shapes=[
            pltpu.SMEM(alignment.shape, jnp.int32),
            pltpu.VMEM(diffusion_mask.shape, jnp.int32),
            pltpu.VMEM((2, BLK, width), jnp.bfloat16),
            pltpu.VMEM((3, 2, BLK, width), jnp.bfloat16),
            pltpu.VMEM((BLK, LANES), jnp.float32),
            pltpu.VMEM((3, chunks, 2 * heads, BLK), jnp.float32),
            pltpu.VMEM((3, chunks, 2 * heads, BLK), jnp.float32),
            pltpu.SemaphoreType.DMA((2,)),
            pltpu.SemaphoreType.DMA((2, 2, width // OWN)),
            pltpu.SemaphoreType.DMA((2, 2, width // OWN)),
            pltpu.SemaphoreType.DMA((chunks,)),
            pltpu.SemaphoreType.DMA((chunks,)),
            pltpu.SemaphoreType.DMA((3, chunks)),
            pltpu.SemaphoreType.DMA((3, chunks)),
            pltpu.SemaphoreType.DMA((2,)),
        ],
        compiler_params=pltpu.CompilerParams(
            collective_id=0, has_side_effects=True, vmem_limit_bytes=24 << 20,
        ),
    )(
        kept(alignment),
        source_length,
        target_length,
        kept(diffusion_mask),
        kept(first_rows),
        kept(second_rows),
    )
    return pl.pallas_call(
        store,
        out_shape=(shape, shape),
        in_specs=[on_chip, on_chip],
        out_specs=(anywhere, anywhere),
        scratch_shapes=[pltpu.SemaphoreType.DMA((2,))],
        compiler_params=pltpu.CompilerParams(vmem_limit_bytes=4 << 20),
    )(*made)


def solution(mesh):
    placed = (
        P("section", "sample", "seq", None),
        P("section", "sample", "seq", None),
        P("sample", "seq", None),
        P("sample", "seq"),
        P("sample"),
        P("sample"),
    )
    return jax.shard_map(
        on_device,
        mesh=mesh,
        in_specs=placed,
        out_specs=(P("section", "sample", "seq", None), P("section", "sample", "seq", None)),
        check_vma=False,
    )
```
